256 devices in a mesh: aux: 16 (over x, z_hi), pair: 16 (over y, z_lo, core).
Axes of the slice: x: 4, y: 4, z: 8 (z_hi: 4, z_lo: 2; z = z_hi * 2 + z_lo), core: 2. Of those that a mesh axis runs over, the one named last changes fastest.
Arguments:
- amplitudes: bfloat16 [512, 36864], P(('aux', 'pair')), may hold values from -6 to 6
- factors: bfloat16 [256, 36864], P('aux'), may hold values from -0.109375 to 0.109375
- sources: int32 [512, 8], P(('aux', 'pair')), may hold values from 0 to 511, as said below
- weights: float32 [512, 8], P(('aux', 'pair')), may hold values from -0.5 to 0.5
- flip_flags: int32 [512, 8], P(('aux', 'pair')), may hold values 0 or 1
Outputs:
- residual: float32 [512, 36864], P(('aux', 'pair'))
The draws below stay inside these ranges and needn't reach their ends.
Inputs may be any that keep to these rules, and one draw needn't show every extreme that they name: `sources`: every source lies in the same aligned block of 32 pairs as its target pair.
All inputs are finite; a program needn't handle non-finite values. No bound on the sum of `flip_flags` on one device may be relied on, other than what follows from the above.
Results may differ from the reference program's by a relative error of at most 0.0026.
Values may be sent and summed in bfloat16 or wider, within the bound.
No kernel may reach another device: no remote copies, remote signals or barrier semaphores. Data moves between devices by JAX's collectives and lax.ppermute only.
A program may use at most 128 MiB of HBM per device.

```python
import jax
import jax.numpy as jnp
from jax import lax

V = 192
NAUX = 256
K = 8
GROUP = 32
NPAIR = 512


def draw_sources(key, part):
    base_ids = jnp.arange(NPAIR, dtype=jnp.int32) // GROUP * GROUP
    offsets = jax.random.randint(key, (NPAIR, K), 0, GROUP, dtype=jnp.int32)
    offsets = offsets.at[NPAIR - 1, 0].set(GROUP - 1)
    offsets = offsets.at[0, 0].set(0)
    return base_ids[:, None] + offsets


def place_ends(drawn, stream_key, least, largest):
    longest = drawn.shape.index(max(drawn.shape))
    spots = []
    for shift in (0, 1):
        where = [jax.random.randint(jax.random.fold_in(stream_key, axis), (), 0, length) for axis, length in enumerate(drawn.shape)]
        where[longest] = (where[longest] + shift) % drawn.shape[longest]
        spots.append(tuple(where))
    return drawn.at[spots[0]].set(least).at[spots[1]].set(largest)


def steps_of(rng, dims, cuts, low, high):
    loudness = 1.0
    for position, shards_of in cuts:
        draws = jax.random.uniform(jax.random.fold_in(jax.random.fold_in(rng, 6), position), (shards_of,), jnp.float32, low / len(cuts), high / len(cuts))
        loudness = loudness * jnp.repeat(jnp.exp(draws), dims[position] // shards_of).reshape((-1,) + (1,) * (len(dims) - 1 - position))
    return loudness


def gaussian(own_key, shape, spread, bound, cuts=(), kind=jnp.bfloat16):
    entries = jax.random.normal(own_key, shape, jnp.float32) * spread
    if len(cuts) > 0:
        entries = steps_of(own_key, shape, cuts, -0.22, 0.18) * entries
    return jnp.clip(entries, min=-bound, max=bound).astype(kind)


def setup_inputs(seed: int = 0) -> dict:
    splits = jax.random.split(jax.random.key(seed), 6)
    amplitudes = gaussian(splits[0], (NPAIR, V * V), 1.0, 6.0, ((0, 256),))
    factors = gaussian(splits[1], (NAUX, V * V), (V * 16) ** -0.5, 0.109375, ((0, 16),))
    sources = draw_sources(jax.random.fold_in(splits[5], 71), 0)
    weights = jnp.clip(jax.random.uniform(splits[3], (NPAIR, K), jnp.float32, -0.5, 0.5) * steps_of(splits[3], (NPAIR, K), ((0, 256),), -0.4, 0.0), -0.5, 0.5)
    flip_flags = place_ends((jax.random.randint(splits[4], (NPAIR, K), 0, 2) < 1).astype(jnp.int32), jax.random.fold_in(splits[4], 1), 0, 1)
    return {"amplitudes": amplitudes, "factors": factors, "sources": sources, "weights": weights, "flip_flags": flip_flags}


def reference(amplitudes, factors, sources, weights, flip_flags):
    amp_full = amplitudes.astype(jnp.float32).reshape(NPAIR, V, V)
    fac_full = factors.astype(jnp.float32).reshape(NAUX, V, V)
    stacked = fac_full.reshape(NAUX // 2, 2, V, V)

    def advance(running, factor_set):
        halfway = jnp.einsum("qab,pbc->pqac", factor_set, amp_full)
        halfway = lax.optimization_barrier(halfway.astype(jnp.bfloat16)).astype(jnp.float32)
        return running + jnp.einsum("pqac,qdc->pad", halfway, factor_set), None

    ladder, unused = lax.scan(advance, jnp.zeros((NPAIR, V, V), jnp.float32), stacked)

    def couple(running, slot_index):
        picked = amp_full[sources[:, slot_index]]
        turned = jnp.swapaxes(picked, 1, 2)
        chosen = jnp.where(flip_flags[:, slot_index][:, None, None] == 1, turned, picked)
        return running + weights[:, slot_index][:, None, None] * chosen, None

    coupling, unused_two = lax.scan(couple, jnp.zeros((NPAIR, V, V), jnp.float32), jnp.arange(K, dtype=jnp.int32))
    return (ladder + coupling).reshape(NPAIR, V * V)
```

```python
import jax
import jax.numpy as jnp
from jax import lax
from jax.experimental import pallas as pl
from jax.experimental.pallas import tpu as pltpu
from jax.sharding import PartitionSpec as P


V = 192
W = 2 * V
TILES = V * V // 128
X, ZH, Y, ZL, C = 4, 4, 4, 2, 2


VMEM = pl.BlockSpec(memory_space=pltpu.VMEM)
SMEM = pl.BlockSpec(memory_space=pltpu.SMEM)


def params(mib):
    return pltpu.CompilerParams(vmem_limit_bytes=mib << 20)


def cost(flops, bytes_accessed):
    return pl.CostEstimate(flops=flops, bytes_accessed=bytes_accessed, transcendentals=0)


def aux_shift(dx, dz):
    return [(x * ZH + z, (x + dx) % X * ZH + (z + dz) % ZH) for x in range(X) for z in range(ZH)]


def pair_flip(mask):
    return [(p, p ^ mask) for p in range(Y * ZL * C)]


def turn(tile):
    return jnp.concatenate([tile[:, 64:], tile[:, :64]], axis=1)


def low_lanes(rows):
    return lax.broadcasted_iota(jnp.int32, (rows, 128), 1) < 64


def prep_kernel(core_ref, amp_ref, fac_ref, pack_ref, own_ref, other_ref, amp_flat, fac_flat, lines):
    half = V // 2
    low = low_lanes(half)
    for k in range(TILES):
        amp_flat[8 * k : 8 * k + 2, :] = amp_ref[:, 128 * k : 128 * k + 128].astype(jnp.float32)
    for k in range(TILES):
        fac_flat[16 * k : 16 * k + 16, :] = fac_ref[:, 128 * k : 128 * k + 128].astype(jnp.float32)

    def write(source, pitch, first, slot, put):
        def strip(row, j):
            return source[pl.ds(pitch * j + row, half, stride=3 * pitch), :]

        for side in range(2):
            s1, s2 = turn(strip(first + side, 1)), turn(strip(first + side, 2))
            lines[slot, side, pl.ds(0, half, stride=2), :] = strip(first + side, 0)
            lines[slot, side, pl.ds(1, half, stride=2), :] = jnp.where(low, s1, s2)
        lines[slot, 2, pl.ds(0, half, stride=2), :] = jnp.where(
            low, strip(first, 1), turn(strip(first + 1, 1))
        )
        lines[slot, 2, pl.ds(1, half, stride=2), :] = jnp.where(
            low, turn(strip(first, 2)), strip(first + 1, 2)
        )
        for t in range(3):
            put(t, lines[slot, t].astype(jnp.bfloat16))

    def put_amp(t, value):
        pack_ref[:, 128 * t : 128 * t + 128] = value

    write(amp_flat, 8, 0, 0, put_amp)
    core = core_ref[0]
    for place, target in ((core, own_ref), (1 - core, other_ref)):
        for q in range(4):

            def put(t, value, target=target, q=q):
                target[q, :, 128 * t : 128 * t + 128] = value

            write(fac_flat, 16, 8 * place + 2 * q, (q + 1) % 4, put)


def prep(core, amplitudes, factors):
    packs = jax.ShapeDtypeStruct((4, V, W), jnp.bfloat16)
    return pl.pallas_call(
        prep_kernel,
        out_shape=(jax.ShapeDtypeStruct((V, W), jnp.bfloat16), packs, packs),
        in_specs=[SMEM, VMEM, VMEM],
        out_specs=(VMEM, VMEM, VMEM),
        scratch_shapes=[
            pltpu.VMEM((8 * TILES, 128), jnp.float32),
            pltpu.VMEM((16 * TILES, 128), jnp.float32),
            pltpu.VMEM((4, 3, V, 128), jnp.float32),
        ],
        compiler_params=params(16),
        cost_estimate=cost(0, 8 << 20),
        name="prep",
    )(core, amplitudes, factors)


def ladder_step(amps, facs, add, low):
    stacked_even = jnp.concatenate(
        [jnp.concatenate([f[:, 0:128], f[:, 256:320]], axis=1) for f in facs], axis=0
    )
    stacked_odd = jnp.concatenate(
        [jnp.concatenate([f[:, 128:256], f[:, 320:384]], axis=1) for f in facs], axis=0
    )
    wide = jnp.concatenate(amps, axis=1)
    even = jnp.dot(stacked_even, wide, preferred_element_type=jnp.float32).astype(jnp.bfloat16)
    odd = jnp.dot(stacked_odd, wide, preferred_element_type=jnp.float32).astype(jnp.bfloat16)
    rows = []
    for p in range(len(amps)):
        first, second = [], []
        for q in range(len(facs)):
            e = even[q * V : (q + 1) * V, p * W : (p + 1) * W]
            o = odd[q * V : (q + 1) * V, p * W : (p + 1) * W]
            first += [e[:, 0:128], o[:, 0:128], jnp.where(low, e[:, 256:], turn(o[:, 256:]))]
            second += [e[:, 128:256], o[:, 128:256], jnp.where(low, turn(e[:, 256:]), o[:, 256:])]
        rows += [jnp.concatenate(first, axis=1), jnp.concatenate(second, axis=1)]
    halfway = jnp.concatenate(rows, axis=0)
    turned = jnp.concatenate(facs, axis=1)
    out = lax.dot_general(
        halfway, turned, (((1,), (1,)), ((), ())), preferred_element_type=jnp.float32
    )
    for p in range(len(amps)):
        a, b = out[2 * p * V : (2 * p + 1) * V], out[(2 * p + 1) * V : (2 * p + 2) * V]
        add(p, 0, a[:, 0:128])
        add(p, 1, b[:, 0:128])
        add(p, 2, jnp.concatenate([a[:, 128:V], b[:, 128:V]], axis=1))


def ladder(amps, facs, carried, first, narrow, deep, name):
    count, arrays = len(amps), len(facs)
    has = carried is not None

    def kernel(*refs):
        amp_refs, fac_refs = refs[:count], refs[count : count + arrays]
        rest = refs[count + arrays :]
        total = rest[-1]
        low = low_lanes(V)
        for p in range(count):
            total[p] = rest[0][first + p] if has else jnp.zeros((V, W), jnp.float32)

        def add(p, t, value):
            total[p, :, 128 * t : 128 * t + 128] += value

        for fac in fac_refs:

            def step(s, none, fac=fac):
                ladder_step([a[...] for a in amp_refs], [fac[s * deep + i] for i in range(deep)], add, low)
                return none

            if deep == 4:
                step(0, 0)
            else:
                lax.fori_loop(0, 4 // deep, step, 0)
        if narrow:
            for p in range(count):
                rest[int(has) + p][...] = total[p].astype(jnp.bfloat16)

    if narrow:
        shapes = tuple(jax.ShapeDtypeStruct((V, W), jnp.bfloat16) for _ in range(count))
        specs, scratch = (VMEM,) * count, [pltpu.VMEM((count, V, W), jnp.float32)]
    else:
        shapes, specs, scratch = jax.ShapeDtypeStruct((count, V, W), jnp.float32), VMEM, []
    operands = [*amps, *facs] + ([carried] if has else [])
    return pl.pallas_call(
        kernel,
        out_shape=shapes,
        in_specs=[VMEM] * len(operands),
        out_specs=specs,
        scratch_shapes=scratch,
        compiler_params=params(24),
        cost_estimate=cost(count * arrays * 16 * 4 * V**3 * 2, 1 << 20),
        name=name,
    )(*operands)


def couple_kernel(where_ref, sources_ref, weights_ref, flips_ref, near_ref, far_ref, out_ref, sums):
    sums[...] = jnp.zeros_like(sums)
    lane = lax.broadcasted_iota(jnp.int32, (V, 128), 1)

    def slot(s, none):
        p, k = s // 8, s % 8
        local = lax.rem(sources_ref[p, k], 2 * Y * ZL * C)
        side = lax.rem(local, 2)
        apart = (local // 2) ^ where_ref[0]
        core, rest = lax.rem(apart, 2), apart // 2
        flip = flips_ref[p, k]
        weight = weights_ref[p, k]
        mixed = jnp.where((lane // 64) == side, weight, 0.0)

        def gather(ref):
            main = ref[rest, :, pl.ds(pl.multiple_of(side * 128, 128), 128)].astype(jnp.float32)
            shared = ref[rest, :, 256:384].astype(jnp.float32)
            sums[p, flip, 0, 0:V, :] += weight * main
            sums[p, flip, 1, 0:V, :] += mixed * shared

        @pl.when(core == 0)
        def _():
            gather(near_ref)

        @pl.when(core == 1)
        def _():
            gather(far_ref)

        return none

    lax.fori_loop(0, 16, slot, 0)
    shared = []
    for p in range(2):
        plain, tail = sums[p, 0, 0, 0:V, :], sums[p, 0, 1, 0:V, :]
        tail = tail + turn(tail)
        turned_tail = sums[p, 1, 1]
        top = sums[p, 1, 0].T
        bottom = (turned_tail + turn(turned_tail)).T
        out_ref[0:128, 128 * p : 128 * p + 128] = plain[0:128] + top[:, 0:128]
        out_ref[128:V, 128 * p : 128 * p + 128] = plain[128:V] + bottom[0:64, 0:128]
        right = jnp.concatenate([top[:, 128:256], bottom[0:64, 128:256]], axis=0)
        shared.append(tail + (right if p == 0 else turn(right)))
    out_ref[:, 256:384] = jnp.where(lane < 64, shared[0], shared[1])


def couple(where, sources, weights, flips, near, far):
    return pl.pallas_call(
        couple_kernel,
        out_shape=jax.ShapeDtypeStruct((V, W), jnp.float32),
        in_specs=[SMEM] * 4 + [VMEM] * 2,
        out_specs=VMEM,
        scratch_shapes=[pltpu.VMEM((2, 2, 2, 256, 128), jnp.float32)],
        compiler_params=params(12),
        cost_estimate=cost(1 << 20, 4 << 20),
        name="couple",
    )(where, sources, weights, flips, near, far)


def finish_kernel(own_ref, couple_ref, a_ref, b_ref, c_ref, out_ref, total, flat):
    half = V // 2
    low = low_lanes(half)
    for t in range(3):
        cut = slice(128 * t, 128 * t + 128)
        total[t] = (own_ref[0, :, cut] + couple_ref[:, cut]) + (
            (a_ref[:, cut].astype(jnp.float32) + b_ref[:, cut].astype(jnp.float32))
            + c_ref[:, cut].astype(jnp.float32)
        )

    def line(t, odd):
        return total[t, pl.ds(odd, half, stride=2), :]

    for p in range(2):
        even, odd = line(2, 0), line(2, 1)
        main = turn(line(p, 1))
        flat[pl.ds(p, half, stride=24), :] = line(p, 0)
        flat[pl.ds(8 + p, half, stride=24), :] = jnp.where(low, even if p == 0 else turn(even), main)
        flat[pl.ds(16 + p, half, stride=24), :] = jnp.where(low, main, turn(odd) if p == 0 else odd)
    for k in range(TILES):
        out_ref[:, 128 * k : 128 * k + 128] = flat[8 * k : 8 * k + 2, :]


def finish(own, coupled, parts):
    return pl.pallas_call(
        finish_kernel,
        out_shape=jax.ShapeDtypeStruct((2, V * V), jnp.float32),
        in_specs=[VMEM] * 5,
        out_specs=VMEM,
        scratch_shapes=[
            pltpu.VMEM((3, V, 128), jnp.float32),
            pltpu.VMEM((8 * TILES, 128), jnp.float32),
        ],
        compiler_params=params(12),
        cost_estimate=cost(1 << 20, 2 << 20),
        name="finish",
    )(own, coupled, *parts)


def local(amplitudes, factors, sources, weights, flips):
    where = lax.axis_index("pair").astype(jnp.int32).reshape(1)
    pack, own, other = prep(where % C, amplitudes, factors)

    def aux(value, dx, dz):
        return lax.ppermute(value, "aux", aux_shift(dx, dz))

    def pair(value, mask):
        return lax.ppermute(value, "pair", pair_flip(mask))

    below, above, across = aux(pack, 0, 1), aux(pack, 0, 3), aux(pack, 0, 2)
    left, right, facing = aux(own, 1, 0), aux(own, 3, 0), aux(own, 2, 0)
    left_other, right_other, facing_other = pair(left, 1), pair(right, 1), pair(facing, 1)

    mates = jnp.stack([pack, pair(pack, 2)])
    mates = jnp.concatenate([mates, pair(mates, 4)])
    near = jnp.concatenate([mates, pair(mates, 8)])
    far = pair(near, 1)

    amps = [below, above, across, pack]
    total = ladder(amps, [own, other], None, 0, False, 2, "ladder_own")
    total = ladder(amps, [left, left_other, right, right_other], total, 0, False, 2, "ladder_side")
    back = ladder(amps[:3], [facing, facing_other], total, 0, True, 4, "ladder_back")
    parts = (aux(back[0], 0, 3), aux(back[1], 0, 1), aux(back[2], 0, 2))
    mine = ladder(amps[3:], [facing, facing_other], total, 3, False, 4, "ladder_mine")
    coupled = couple(where, sources, weights, flips, near, far)
    return finish(mine, coupled, parts)


def solution(mesh):
    placed = (
        P(("aux", "pair"), None),
        P("aux", None),
        P(("aux", "pair"), None),
        P(("aux", "pair"), None),
        P(("aux", "pair"), None),
    )
    return jax.shard_map(
        local, mesh=mesh, in_specs=placed, out_specs=P(("aux", "pair"), None), check_vma=False
    )
```

```python
import jax
import jax.numpy as jnp
from jax import lax
from jax.experimental import pallas as pl
from jax.experimental.pallas import tpu as pltpu
from jax.sharding import PartitionSpec as P


V = 192
W = 2 * V
TILES = V * V // 128
X, ZH, Y, ZL, C = 4, 4, 4, 2, 2


VMEM = pl.BlockSpec(memory_space=pltpu.VMEM)
SMEM = pl.BlockSpec(memory_space=pltpu.SMEM)


def params(mib):
    return pltpu.CompilerParams(vmem_limit_bytes=mib << 20)


def cost(flops, bytes_accessed):
    return pl.CostEstimate(flops=flops, bytes_accessed=bytes_accessed, transcendentals=0)


def aux_shift(dx, dz):
    return [(x * ZH + z, (x + dx) % X * ZH + (z + dz) % ZH) for x in range(X) for z in range(ZH)]


def pair_flip(mask):
    return [(p, p ^ mask) for p in range(Y * ZL * C)]


def turn(tile):
    return jnp.concatenate([tile[:, 64:], tile[:, :64]], axis=1)


def low_lanes(rows):
    return lax.broadcasted_iota(jnp.int32, (rows, 128), 1) < 64


def write_pack(source, pitch, first, lines, put):
    half = V // 2
    low = low_lanes(half)

    def strip(row, j):
        return source[pl.ds(pitch * j + row, half, stride=3 * pitch), :]

    for side in range(2):
        s1, s2 = turn(strip(first + side, 1)), turn(strip(first + side, 2))
        lines[side, pl.ds(0, half, stride=2), :] = strip(first + side, 0)
        lines[side, pl.ds(1, half, stride=2), :] = jnp.where(low, s1, s2)
    lines[2, pl.ds(0, half, stride=2), :] = jnp.where(low, strip(first, 1), turn(strip(first + 1, 1)))
    lines[2, pl.ds(1, half, stride=2), :] = jnp.where(low, turn(strip(first, 2)), strip(first + 1, 2))
    for t in range(3):
        put(t, lines[t].astype(jnp.bfloat16))


def prep_amp_kernel(amp_ref, pack_ref, flat, lines):
    for k in range(TILES):
        flat[8 * k : 8 * k + 2, :] = amp_ref[:, 128 * k : 128 * k + 128].astype(jnp.float32)

    def put(t, value):
        pack_ref[:, 128 * t : 128 * t + 128] = value

    write_pack(flat, 8, 0, lines, put)


def prep_fac_kernel(core_ref, fac_ref, own_ref, other_ref, flat, lines):
    for k in range(TILES):
        flat[16 * k : 16 * k + 16, :] = fac_ref[:, 128 * k : 128 * k + 128].astype(jnp.float32)
    core = core_ref[0]
    for place, target in ((core, own_ref), (1 - core, other_ref)):
        for q in range(4):

            def put(t, value, target=target, q=q):
                target[q, :, 128 * t : 128 * t + 128] = value

            write_pack(flat, 16, 8 * place + 2 * q, lines.at[q], put)


def prep_amp(amplitudes):
    return pl.pallas_call(
        prep_amp_kernel,
        out_shape=jax.ShapeDtypeStruct((V, W), jnp.bfloat16),
        in_specs=[VMEM],
        out_specs=VMEM,
        scratch_shapes=[
            pltpu.VMEM((8 * TILES, 128), jnp.float32),
            pltpu.VMEM((3, V, 128), jnp.float32),
        ],
        compiler_params=params(12),
        cost_estimate=cost(0, 2 << 20),
        name="prep_amp",
    )(amplitudes)


def prep_fac(core, factors):
    packs = jax.ShapeDtypeStruct((4, V, W), jnp.bfloat16)
    return pl.pallas_call(
        prep_fac_kernel,
        out_shape=(packs, packs),
        in_specs=[SMEM, VMEM],
        out_specs=(VMEM, VMEM),
        scratch_shapes=[
            pltpu.VMEM((16 * TILES, 128), jnp.float32),
            pltpu.VMEM((4, 3, V, 128), jnp.float32),
        ],
        compiler_params=params(16),
        cost_estimate=cost(0, 6 << 20),
        name="prep_fac",
    )(core, factors)


def ladder_step(amps, facs, add, low):
    stacked_even = jnp.concatenate(
        [jnp.concatenate([f[:, 0:128], f[:, 256:320]], axis=1) for f in facs], axis=0
    )
    stacked_odd = jnp.concatenate(
        [jnp.concatenate([f[:, 128:256], f[:, 320:384]], axis=1) for f in facs], axis=0
    )
    wide = jnp.concatenate(amps, axis=1)
    even = jnp.dot(stacked_even, wide, preferred_element_type=jnp.float32).astype(jnp.bfloat16)
    odd = jnp.dot(stacked_odd, wide, preferred_element_type=jnp.float32).astype(jnp.bfloat16)
    rows = []
    for p in range(len(amps)):
        first, second = [], []
        for q in range(len(facs)):
            e = even[q * V : (q + 1) * V, p * W : (p + 1) * W]
            o = odd[q * V : (q + 1) * V, p * W : (p + 1) * W]
            first += [e[:, 0:128], o[:, 0:128], jnp.where(low, e[:, 256:], turn(o[:, 256:]))]
            second += [e[:, 128:256], o[:, 128:256], jnp.where(low, turn(e[:, 256:]), o[:, 256:])]
        rows += [jnp.concatenate(first, axis=1), jnp.concatenate(second, axis=1)]
    halfway = jnp.concatenate(rows, axis=0)
    turned = jnp.concatenate(facs, axis=1)
    out = lax.dot_general(
        halfway, turned, (((1,), (1,)), ((), ())), preferred_element_type=jnp.float32
    )
    for p in range(len(amps)):
        a, b = out[2 * p * V : (2 * p + 1) * V], out[(2 * p + 1) * V : (2 * p + 2) * V]
        add(p, 0, a[:, 0:128])
        add(p, 1, b[:, 0:128])
        add(p, 2, jnp.concatenate([a[:, 128:V], b[:, 128:V]], axis=1))


def ladder(amps, facs, carried, narrow, deep):
    count, arrays = len(amps), sum(f.shape[0] // 4 for f in facs)
    held = []
    for array, _ in carried:
        if not any(array is h for h in held):
            held.append(array)
    places = [([array is h for h in held].index(True), at) for array, at in carried]
    ins = count + len(facs) + len(held)

    def kernel(*refs):
        amp_refs, fac_refs = refs[:count], refs[count : count + len(facs)]
        held_refs, outs = refs[count + len(facs) : ins], refs[ins:]
        total = outs[-1]
        low = low_lanes(V)
        for p in range(count):
            if places:
                total[p] = held_refs[places[p][0]][places[p][1]]
            else:
                total[p] = jnp.zeros((V, W), jnp.float32)

        def add(p, t, value):
            total[p, :, 128 * t : 128 * t + 128] += value

        for fac in fac_refs:

            def step(s, none, fac=fac):
                ladder_step([a[...] for a in amp_refs], [fac[s * deep + i] for i in range(deep)], add, low)
                return none

            lax.fori_loop(0, fac.shape[0] // deep, step, 0)
        if narrow:
            for p in range(count):
                outs[p][...] = total[p].astype(jnp.bfloat16)

    if narrow:
        shapes = tuple(jax.ShapeDtypeStruct((V, W), jnp.bfloat16) for _ in range(count))
        specs, scratch = (VMEM,) * count, [pltpu.VMEM((count, V, W), jnp.float32)]
    else:
        shapes, specs, scratch = jax.ShapeDtypeStruct((count, V, W), jnp.float32), VMEM, []
    return pl.pallas_call(
        kernel,
        out_shape=shapes,
        in_specs=[VMEM] * ins,
        out_specs=specs,
        scratch_shapes=scratch,
        compiler_params=params(24),
        cost_estimate=cost(count * arrays * 16 * 4 * V**3 * 2, 1 << 20),
    )(*amps, *facs, *held)


def couple_kernel(where_ref, sources_ref, weights_ref, flips_ref, near_ref, far_ref, out_ref, sums):
    sums[...] = jnp.zeros_like(sums)
    lane = lax.broadcasted_iota(jnp.int32, (V, 128), 1)

    def slot(s, none):
        p, k = s // 8, s % 8
        local = lax.rem(sources_ref[p, k], 2 * Y * ZL * C)
        side = lax.rem(local, 2)
        apart = (local // 2) ^ where_ref[0]
        core, rest = lax.rem(apart, 2), apart // 2
        flip = flips_ref[p, k]
        weight = weights_ref[p, k]
        mixed = jnp.where((lane // 64) == side, weight, 0.0)

        def gather(ref):
            main = ref[rest, :, pl.ds(pl.multiple_of(side * 128, 128), 128)].astype(jnp.float32)
            shared = ref[rest, :, 256:384].astype(jnp.float32)
            sums[p, flip, 0, 0:V, :] += weight * main
            sums[p, flip, 1, 0:V, :] += mixed * shared

        @pl.when(core == 0)
        def _():
            gather(near_ref)

        @pl.when(core == 1)
        def _():
            gather(far_ref)

        return none

    lax.fori_loop(0, 16, slot, 0)
    shared = []
    for p in range(2):
        plain, tail = sums[p, 0, 0, 0:V, :], sums[p, 0, 1, 0:V, :]
        tail = tail + turn(tail)
        turned_tail = sums[p, 1, 1]
        top = sums[p, 1, 0].T
        bottom = (turned_tail + turn(turned_tail)).T
        out_ref[0:128, 128 * p : 128 * p + 128] = plain[0:128] + top[:, 0:128]
        out_ref[128:V, 128 * p : 128 * p + 128] = plain[128:V] + bottom[0:64, 0:128]
        right = jnp.concatenate([top[:, 128:256], bottom[0:64, 128:256]], axis=0)
        shared.append(tail + (right if p == 0 else turn(right)))
    out_ref[:, 256:384] = jnp.where(lane < 64, shared[0], shared[1])


def couple(where, sources, weights, flips, near, far):
    return pl.pallas_call(
        couple_kernel,
        out_shape=jax.ShapeDtypeStruct((V, W), jnp.float32),
        in_specs=[SMEM] * 4 + [VMEM] * 2,
        out_specs=VMEM,
        scratch_shapes=[pltpu.VMEM((2, 2, 2, 256, 128), jnp.float32)],
        compiler_params=params(12),
        cost_estimate=cost(1 << 20, 4 << 20),
        name="couple",
    )(where, sources, weights, flips, near, far)


def finish_kernel(own_ref, couple_ref, a_ref, b_ref, c_ref, out_ref, total, flat):
    half = V // 2
    low = low_lanes(half)
    for t in range(3):
        cut = slice(128 * t, 128 * t + 128)
        total[t] = (own_ref[0, :, cut] + couple_ref[:, cut]) + (
            (a_ref[:, cut].astype(jnp.float32) + b_ref[:, cut].astype(jnp.float32))
            + c_ref[:, cut].astype(jnp.float32)
        )

    def line(t, odd):
        return total[t, pl.ds(odd, half, stride=2), :]

    for p in range(2):
        even, odd = line(2, 0), line(2, 1)
        main = turn(line(p, 1))
        flat[pl.ds(p, half, stride=24), :] = line(p, 0)
        flat[pl.ds(8 + p, half, stride=24), :] = jnp.where(low, even if p == 0 else turn(even), main)
        flat[pl.ds(16 + p, half, stride=24), :] = jnp.where(low, main, turn(odd) if p == 0 else odd)
    for k in range(TILES):
        out_ref[:, 128 * k : 128 * k + 128] = flat[8 * k : 8 * k + 2, :]


def finish(own, coupled, parts):
    return pl.pallas_call(
        finish_kernel,
        out_shape=jax.ShapeDtypeStruct((2, V * V), jnp.float32),
        in_specs=[VMEM] * 5,
        out_specs=VMEM,
        scratch_shapes=[
            pltpu.VMEM((3, V, 128), jnp.float32),
            pltpu.VMEM((8 * TILES, 128), jnp.float32),
        ],
        compiler_params=params(12),
        cost_estimate=cost(1 << 20, 2 << 20),
        name="finish",
    )(own, coupled, *parts)


def local(amplitudes, factors, sources, weights, flips):
    where = lax.axis_index("pair").astype(jnp.int32).reshape(1)

    def aux(value, dx, dz):
        return lax.ppermute(value, "aux", aux_shift(dx, dz))

    def pair(value, mask):
        return lax.ppermute(value, "pair", pair_flip(mask))

    pack = prep_amp(amplitudes)
    across, below, above = aux(pack, 0, 2), aux(pack, 0, 1), aux(pack, 0, 3)
    own, other = prep_fac(where % C, factors)
    left, right = aux(own, 1, 0), aux(own, 3, 0)
    self_total = ladder([pack], [own, other], [], False, 4)
    facing = aux(own, 2, 0)
    mates = jnp.stack([pack, pair(pack, 2)])
    rest = [across, below, above]
    total = ladder(rest, [own, other], [], False, 4)
    mates = jnp.concatenate([mates, pair(mates, 4)])
    sides_other = pair(jnp.concatenate([left, right]), 1)
    carried = [(total, 0), (total, 1), (total, 2), (self_total, 0)]
    total4 = ladder(rest + [pack], [left, right], carried, False, 2)
    near = jnp.concatenate([mates, pair(mates, 8)])
    total = ladder(rest, [sides_other], [(total4, i) for i in range(3)], False, 4)
    facing_other = pair(facing, 1)
    total = ladder(rest, [facing], [(total, i) for i in range(3)], False, 4)
    far = pair(near, 1)
    back = ladder(rest, [facing_other], [(total, i) for i in range(3)], True, 4)
    parts = (aux(back[0], 0, 2), aux(back[1], 0, 3), aux(back[2], 0, 1))
    mine = ladder([pack], [sides_other, facing, facing_other], [(total4, 3)], False, 4)
    coupled = couple(where, sources, weights, flips, near, far)
    return finish(mine, coupled, parts)


def solution(mesh):
    placed = (
        P(("aux", "pair"), None),
        P("aux", None),
        P(("aux", "pair"), None),
        P(("aux", "pair"), None),
        P(("aux", "pair"), None),
    )
    return jax.shard_map(
        local, mesh=mesh, in_specs=placed, out_specs=P(("aux", "pair"), None), check_vma=False
    )
```

```python
import jax
import jax.numpy as jnp
from jax import lax
from jax.experimental import pallas as pl
from jax.experimental.pallas import tpu as pltpu
from jax.sharding import PartitionSpec as P


V = 192
W = 2 * V
TILES = V * V // 128
X, ZH, Y, ZL, C = 4, 4, 4, 2, 2


VMEM = pl.BlockSpec(memory_space=pltpu.VMEM)
SMEM = pl.BlockSpec(memory_space=pltpu.SMEM)


def params(mib):
    return pltpu.CompilerParams(vmem_limit_bytes=mib << 20)


def cost(flops, bytes_accessed):
    return pl.CostEstimate(flops=flops, bytes_accessed=bytes_accessed, transcendentals=0)


def aux_flip(mask):
    return [(a, a ^ mask) for a in range(X * ZH)]


def pair_flip(mask):
    return [(p, p ^ mask) for p in range(Y * ZL * C)]


def turn(tile):
    return jnp.concatenate([tile[:, 64:], tile[:, :64]], axis=1)


def low_lanes(rows):
    return lax.broadcasted_iota(jnp.int32, (rows, 128), 1) < 64


def write_pack(source, pitch, first, lines, put):
    half = V // 2
    low = low_lanes(half)

    def strip(row, j):
        return source[pl.ds(pitch * j + row, half, stride=3 * pitch), :]

    for side in range(2):
        s1, s2 = turn(strip(first + side, 1)), turn(strip(first + side, 2))
        lines[side, pl.ds(0, half, stride=2), :] = strip(first + side, 0)
        lines[side, pl.ds(1, half, stride=2), :] = jnp.where(low, s1, s2)
    lines[2, pl.ds(0, half, stride=2), :] = jnp.where(low, strip(first, 1), turn(strip(first + 1, 1)))
    lines[2, pl.ds(1, half, stride=2), :] = jnp.where(low, turn(strip(first, 2)), strip(first + 1, 2))
    for t in range(3):
        put(t, lines[t].astype(jnp.bfloat16))


def prep_amp_kernel(amp_ref, pack_ref, flat, lines):
    for k in range(TILES):
        flat[8 * k : 8 * k + 2, :] = amp_ref[:, 128 * k : 128 * k + 128].astype(jnp.float32)

    def put(t, value):
        pack_ref[:, 128 * t : 128 * t + 128] = value

    write_pack(flat, 8, 0, lines, put)


def prep_fac_kernel(core_ref, fac_ref, own_ref, other_ref, flat, lines):
    for k in range(TILES):
        flat[16 * k : 16 * k + 16, :] = fac_ref[:, 128 * k : 128 * k + 128].astype(jnp.float32)
    core = core_ref[0]
    for place, target in ((core, own_ref), (1 - core, other_ref)):
        for q in range(4):

            def put(t, value, target=target, q=q):
                target[q, :, 128 * t : 128 * t + 128] = value

            write_pack(flat, 16, 8 * place + 2 * q, lines.at[q], put)


def prep_amp(amplitudes):
    return pl.pallas_call(
        prep_amp_kernel,
        out_shape=jax.ShapeDtypeStruct((V, W), jnp.bfloat16),
        in_specs=[VMEM],
        out_specs=VMEM,
        scratch_shapes=[
            pltpu.VMEM((8 * TILES, 128), jnp.float32),
            pltpu.VMEM((3, V, 128), jnp.float32),
        ],
        compiler_params=params(12),
        cost_estimate=cost(0, 2 << 20),
        name="prep_amp",
    )(amplitudes)


def prep_fac(core, factors):
    packs = jax.ShapeDtypeStruct((4, V, W), jnp.bfloat16)
    return pl.pallas_call(
        prep_fac_kernel,
        out_shape=(packs, packs),
        in_specs=[SMEM, VMEM],
        out_specs=(VMEM, VMEM),
        scratch_shapes=[
            pltpu.VMEM((16 * TILES, 128), jnp.float32),
            pltpu.VMEM((4, 3, V, 128), jnp.float32),
        ],
        compiler_params=params(16),
        cost_estimate=cost(0, 6 << 20),
        name="prep_fac",
    )(core, factors)


def ladder_step(amps, facs, add, low):
    stacked_even = jnp.concatenate(
        [jnp.concatenate([f[:, 0:128], f[:, 256:320]], axis=1) for f in facs], axis=0
    )
    stacked_odd = jnp.concatenate(
        [jnp.concatenate([f[:, 128:256], f[:, 320:384]], axis=1) for f in facs], axis=0
    )
    wide = jnp.concatenate(amps, axis=1)
    even = jnp.dot(stacked_even, wide, preferred_element_type=jnp.float32).astype(jnp.bfloat16)
    odd = jnp.dot(stacked_odd, wide, preferred_element_type=jnp.float32).astype(jnp.bfloat16)
    rows = []
    for p in range(len(amps)):
        first, second = [], []
        for q in range(len(facs)):
            e = even[q * V : (q + 1) * V, p * W : (p + 1) * W]
            o = odd[q * V : (q + 1) * V, p * W : (p + 1) * W]
            first += [e[:, 0:128], o[:, 0:128], jnp.where(low, e[:, 256:], turn(o[:, 256:]))]
            second += [e[:, 128:256], o[:, 128:256], jnp.where(low, turn(e[:, 256:]), o[:, 256:])]
        rows += [jnp.concatenate(first, axis=1), jnp.concatenate(second, axis=1)]
    halfway = jnp.concatenate(rows, axis=0)
    turned = jnp.concatenate(facs, axis=1)
    out = lax.dot_general(
        halfway, turned, (((1,), (1,)), ((), ())), preferred_element_type=jnp.float32
    )
    for p in range(len(amps)):
        a, b = out[2 * p * V : (2 * p + 1) * V], out[(2 * p + 1) * V : (2 * p + 2) * V]
        add(p, 0, a[:, 0:128])
        add(p, 1, b[:, 0:128])
        add(p, 2, jnp.concatenate([a[:, 128:V], b[:, 128:V]], axis=1))


def ladder(amps, facs, carried, narrow, deep):
    count, arrays = len(amps), sum(f.shape[0] // 4 for f in facs)
    held = []
    for array, _ in carried:
        if not any(array is h for h in held):
            held.append(array)
    places = [([array is h for h in held].index(True), at) for array, at in carried]
    ins = count + len(facs) + len(held)

    def kernel(*refs):
        amp_refs, fac_refs = refs[:count], refs[count : count + len(facs)]
        held_refs, outs = refs[count + len(facs) : ins], refs[ins:]
        total = outs[-1]
        low = low_lanes(V)
        for p in range(count):
            if places:
                total[p] = held_refs[places[p][0]][places[p][1]]
            else:
                total[p] = jnp.zeros((V, W), jnp.float32)

        def add(p, t, value):
            total[p, :, 128 * t : 128 * t + 128] += value

        for fac in fac_refs:

            def step(s, none, fac=fac):
                ladder_step([a[...] for a in amp_refs], [fac[s * deep + i] for i in range(deep)], add, low)
                return none

            lax.fori_loop(0, fac.shape[0] // deep, step, 0)
        if narrow:
            for p in range(count):
                outs[p][...] = total[p].astype(jnp.bfloat16)

    if narrow:
        shapes = tuple(jax.ShapeDtypeStruct((V, W), jnp.bfloat16) for _ in range(count))
        specs, scratch = (VMEM,) * count, [pltpu.VMEM((count, V, W), jnp.float32)]
    else:
        shapes, specs, scratch = jax.ShapeDtypeStruct((count, V, W), jnp.float32), VMEM, []
    return pl.pallas_call(
        kernel,
        out_shape=shapes,
        in_specs=[VMEM] * ins,
        out_specs=specs,
        scratch_shapes=scratch,
        compiler_params=params(24),
        cost_estimate=cost(count * arrays * 16 * 4 * V**3 * 2, 1 << 20),
    )(*amps, *facs, *held)


def couple_kernel(where_ref, sources_ref, weights_ref, flips_ref, near_ref, far_ref, out_ref, sums):
    sums[...] = jnp.zeros_like(sums)
    lane = lax.broadcasted_iota(jnp.int32, (V, 128), 1)

    def slot(s, none):
        p, k = s // 8, s % 8
        local = lax.rem(sources_ref[p, k], 2 * Y * ZL * C)
        side = lax.rem(local, 2)
        apart = (local // 2) ^ where_ref[0]
        core, rest = lax.rem(apart, 2), apart // 2
        flip = flips_ref[p, k]
        weight = weights_ref[p, k]
        mixed = jnp.where((lane // 64) == side, weight, 0.0)

        def gather(ref):
            main = ref[rest, :, pl.ds(pl.multiple_of(side * 128, 128), 128)].astype(jnp.float32)
            shared = ref[rest, :, 256:384].astype(jnp.float32)
            sums[p, flip, 0, 0:V, :] += weight * main
            sums[p, flip, 1, 0:V, :] += mixed * shared

        @pl.when(core == 0)
        def _():
            gather(near_ref)

        @pl.when(core == 1)
        def _():
            gather(far_ref)

        return none

    lax.fori_loop(0, 16, slot, 0)
    shared = []
    for p in range(2):
        plain, tail = sums[p, 0, 0, 0:V, :], sums[p, 0, 1, 0:V, :]
        tail = tail + turn(tail)
        turned_tail = sums[p, 1, 1]
        top = sums[p, 1, 0].T
        bottom = (turned_tail + turn(turned_tail)).T
        out_ref[0:128, 128 * p : 128 * p + 128] = plain[0:128] + top[:, 0:128]
        out_ref[128:V, 128 * p : 128 * p + 128] = plain[128:V] + bottom[0:64, 0:128]
        right = jnp.concatenate([top[:, 128:256], bottom[0:64, 128:256]], axis=0)
        shared.append(tail + (right if p == 0 else turn(right)))
    out_ref[:, 256:384] = jnp.where(lane < 64, shared[0], shared[1])


def couple(where, sources, weights, flips, near, far):
    return pl.pallas_call(
        couple_kernel,
        out_shape=jax.ShapeDtypeStruct((V, W), jnp.float32),
        in_specs=[SMEM] * 4 + [VMEM] * 2,
        out_specs=VMEM,
        scratch_shapes=[pltpu.VMEM((2, 2, 2, 256, 128), jnp.float32)],
        compiler_params=params(12),
        cost_estimate=cost(1 << 20, 4 << 20),
        name="couple",
    )(where, sources, weights, flips, near, far)


def finish_kernel(own_ref, couple_ref, a_ref, b_ref, c_ref, out_ref, total, flat):
    half = V // 2
    low = low_lanes(half)
    for t in range(3):
        cut = slice(128 * t, 128 * t + 128)
        total[t] = (own_ref[0, :, cut] + couple_ref[:, cut]) + (
            (a_ref[:, cut].astype(jnp.float32) + b_ref[:, cut].astype(jnp.float32))
            + c_ref[:, cut].astype(jnp.float32)
        )

    def line(t, odd):
        return total[t, pl.ds(odd, half, stride=2), :]

    for p in range(2):
        even, odd = line(2, 0), line(2, 1)
        main = turn(line(p, 1))
        flat[pl.ds(p, half, stride=24), :] = line(p, 0)
        flat[pl.ds(8 + p, half, stride=24), :] = jnp.where(low, even if p == 0 else turn(even), main)
        flat[pl.ds(16 + p, half, stride=24), :] = jnp.where(low, main, turn(odd) if p == 0 else odd)
    for k in range(TILES):
        out_ref[:, 128 * k : 128 * k + 128] = flat[8 * k : 8 * k + 2, :]


def finish(own, coupled, parts):
    return pl.pallas_call(
        finish_kernel,
        out_shape=jax.ShapeDtypeStruct((2, V * V), jnp.float32),
        in_specs=[VMEM] * 5,
        out_specs=VMEM,
        scratch_shapes=[
            pltpu.VMEM((3, V, 128), jnp.float32),
            pltpu.VMEM((8 * TILES, 128), jnp.float32),
        ],
        compiler_params=params(12),
        cost_estimate=cost(1 << 20, 2 << 20),
        name="finish",
    )(own, coupled, *parts)


def local(amplitudes, factors, sources, weights, flips):
    where = lax.axis_index("pair").astype(jnp.int32).reshape(1)

    def aux(value, mask):
        return lax.ppermute(value, "aux", aux_flip(mask))

    def pair(value, mask):
        return lax.ppermute(value, "pair", pair_flip(mask))

    pack = prep_amp(amplitudes)
    across, below, above = aux(pack, 2), aux(pack, 1), aux(pack, 3)
    own, other = prep_fac(where % C, factors)
    left, right = aux(own, ZH), aux(own, 3 * ZH)
    self_total = ladder([pack], [own, other], [], False, 4)
    facing = aux(own, 2 * ZH)
    mates = jnp.stack([pack, pair(pack, 2)])
    rest = [across, below, above]
    total = ladder(rest, [own, other], [], False, 4)
    mates = jnp.concatenate([mates, pair(mates, 4)])
    sides_other = pair(jnp.concatenate([left, right]), 1)
    carried = [(total, 0), (total, 1), (total, 2), (self_total, 0)]
    total4 = ladder(rest + [pack], [left, right], carried, False, 2)
    near = jnp.concatenate([mates, pair(mates, 8)])
    total = ladder(rest, [sides_other], [(total4, i) for i in range(3)], False, 4)
    facing_other = pair(facing, 1)
    total = ladder(rest, [facing], [(total, i) for i in range(3)], False, 4)
    far = pair(near, 1)
    back = ladder(rest, [facing_other], [(total, i) for i in range(3)], True, 4)
    parts = (aux(back[0], 2), aux(back[1], 1), aux(back[2], 3))
    mine = ladder([pack], [sides_other, facing, facing_other], [(total4, 3)], False, 4)
    coupled = couple(where, sources, weights, flips, near, far)
    return finish(mine, coupled, parts)


def solution(mesh):
    placed = (
        P(("aux", "pair"), None),
        P("aux", None),
        P(("aux", "pair"), None),
        P(("aux", "pair"), None),
        P(("aux", "pair"), None),
    )
    return jax.shard_map(
        local, mesh=mesh, in_specs=placed, out_specs=P(("aux", "pair"), None), check_vma=False
    )
```

```python
import jax
import jax.numpy as jnp
from jax import lax
from jax.experimental import pallas as pl
from jax.experimental.pallas import tpu as pltpu
from jax.sharding import PartitionSpec as P


V = 192
W = 2 * V
TILES = V * V // 128
X, ZH, Y, ZL, C = 4, 4, 4, 2, 2


VMEM = pl.BlockSpec(memory_space=pltpu.VMEM)
SMEM = pl.BlockSpec(memory_space=pltpu.SMEM)


def params(mib):
    return pltpu.CompilerParams(vmem_limit_bytes=mib << 20)


def cost(flops, bytes_accessed):
    return pl.CostEstimate(flops=flops, bytes_accessed=bytes_accessed, transcendentals=0)


def aux_flip(mask):
    return [(a, a ^ mask) for a in range(X * ZH)]


def pair_flip(mask):
    return [(p, p ^ mask) for p in range(Y * ZL * C)]


def turn(tile):
    return jnp.concatenate([tile[:, 64:], tile[:, :64]], axis=1)


def low_lanes(rows):
    return lax.broadcasted_iota(jnp.int32, (rows, 128), 1) < 64


def write_pack(source, pitch, first, lines, put):
    half = V // 2
    low = low_lanes(half)

    def strip(row, j):
        return source[pl.ds(pitch * j + row, half, stride=3 * pitch), :]

    for side in range(2):
        s1, s2 = turn(strip(first + side, 1)), turn(strip(first + side, 2))
        lines[side, pl.ds(0, half, stride=2), :] = strip(first + side, 0)
        lines[side, pl.ds(1, half, stride=2), :] = jnp.where(low, s1, s2)
    lines[2, pl.ds(0, half, stride=2), :] = jnp.where(low, strip(first, 1), turn(strip(first + 1, 1)))
    lines[2, pl.ds(1, half, stride=2), :] = jnp.where(low, turn(strip(first, 2)), strip(first + 1, 2))
    for t in range(3):
        put(t, lines[t].astype(jnp.bfloat16))


def prep_amp_kernel(amp_ref, pack_ref, flat, lines):
    for k in range(TILES):
        flat[8 * k : 8 * k + 2, :] = amp_ref[:, 128 * k : 128 * k + 128].astype(jnp.float32)

    def put(t, value):
        pack_ref[:, 128 * t : 128 * t + 128] = value

    write_pack(flat, 8, 0, lines, put)


def prep_fac_kernel(core_ref, fac_ref, own_ref, other_ref, flat, lines):
    for k in range(TILES):
        flat[16 * k : 16 * k + 16, :] = fac_ref[:, 128 * k : 128 * k + 128].astype(jnp.float32)
    core = core_ref[0]
    for place, target in ((core, own_ref), (1 - core, other_ref)):
        for q in range(4):

            def put(t, value, target=target, q=q):
                target[q, :, 128 * t : 128 * t + 128] = value

            write_pack(flat, 16, 8 * place + 2 * q, lines.at[q], put)


def prep_amp(amplitudes):
    return pl.pallas_call(
        prep_amp_kernel,
        out_shape=jax.ShapeDtypeStruct((V, W), jnp.bfloat16),
        in_specs=[VMEM],
        out_specs=VMEM,
        scratch_shapes=[
            pltpu.VMEM((8 * TILES, 128), jnp.float32),
            pltpu.VMEM((3, V, 128), jnp.float32),
        ],
        compiler_params=params(12),
        cost_estimate=cost(0, 2 << 20),
        name="prep_amp",
    )(amplitudes)


def prep_fac(core, factors):
    packs = jax.ShapeDtypeStruct((4, V, W), jnp.bfloat16)
    return pl.pallas_call(
        prep_fac_kernel,
        out_shape=(packs, packs),
        in_specs=[SMEM, VMEM],
        out_specs=(VMEM, VMEM),
        scratch_shapes=[
            pltpu.VMEM((16 * TILES, 128), jnp.float32),
            pltpu.VMEM((4, 3, V, 128), jnp.float32),
        ],
        compiler_params=params(16),
        cost_estimate=cost(0, 6 << 20),
        name="prep_fac",
    )(core, factors)


def ladder_step(amps, facs, add, low):
    stacked_even = jnp.concatenate(
        [jnp.concatenate([f[:, 0:128], f[:, 256:320]], axis=1) for f in facs], axis=0
    )
    stacked_odd = jnp.concatenate(
        [jnp.concatenate([f[:, 128:256], f[:, 320:384]], axis=1) for f in facs], axis=0
    )
    wide = jnp.concatenate(amps, axis=1)
    even = jnp.dot(stacked_even, wide, preferred_element_type=jnp.float32).astype(jnp.bfloat16)
    odd = jnp.dot(stacked_odd, wide, preferred_element_type=jnp.float32).astype(jnp.bfloat16)
    rows = []
    for p in range(len(amps)):
        first, second = [], []
        for q in range(len(facs)):
            e = even[q * V : (q + 1) * V, p * W : (p + 1) * W]
            o = odd[q * V : (q + 1) * V, p * W : (p + 1) * W]
            first += [e[:, 0:128], o[:, 0:128], jnp.where(low, e[:, 256:], turn(o[:, 256:]))]
            second += [e[:, 128:256], o[:, 128:256], jnp.where(low, turn(e[:, 256:]), o[:, 256:])]
        rows += [jnp.concatenate(first, axis=1), jnp.concatenate(second, axis=1)]
    halfway = jnp.concatenate(rows, axis=0)
    turned = jnp.concatenate(facs, axis=1)
    out = lax.dot_general(
        halfway, turned, (((1,), (1,)), ((), ())), preferred_element_type=jnp.float32
    )
    for p in range(len(amps)):
        a, b = out[2 * p * V : (2 * p + 1) * V], out[(2 * p + 1) * V : (2 * p + 2) * V]
        add(p, 0, a[:, 0:128])
        add(p, 1, b[:, 0:128])
        add(p, 2, jnp.concatenate([a[:, 128:V], b[:, 128:V]], axis=1))


def ladder(amps, facs, carried, narrow, deep):
    count, arrays = len(amps), sum(f.shape[0] // 4 for f in facs)
    held = []
    for array, _ in carried:
        if not any(array is h for h in held):
            held.append(array)
    places = [([array is h for h in held].index(True), at) for array, at in carried]
    ins = count + len(facs) + len(held)

    def kernel(*refs):
        amp_refs, fac_refs = refs[:count], refs[count : count + len(facs)]
        held_refs, outs = refs[count + len(facs) : ins], refs[ins:]
        total = outs[-1]
        low = low_lanes(V)
        for p in range(count):
            if places:
                total[p] = held_refs[places[p][0]][places[p][1]]
            else:
                total[p] = jnp.zeros((V, W), jnp.float32)

        def add(p, t, value):
            total[p, :, 128 * t : 128 * t + 128] += value

        for fac in fac_refs:

            def step(s, none, fac=fac):
                ladder_step([a[...] for a in amp_refs], [fac[s * deep + i] for i in range(deep)], add, low)
                return none

            lax.fori_loop(0, fac.shape[0] // deep, step, 0)
        if narrow:
            for p in range(count):
                outs[p][...] = total[p].astype(jnp.bfloat16)

    if narrow:
        shapes = tuple(jax.ShapeDtypeStruct((V, W), jnp.bfloat16) for _ in range(count))
        specs, scratch = (VMEM,) * count, [pltpu.VMEM((count, V, W), jnp.float32)]
    else:
        shapes, specs, scratch = jax.ShapeDtypeStruct((count, V, W), jnp.float32), VMEM, []
    return pl.pallas_call(
        kernel,
        out_shape=shapes,
        in_specs=[VMEM] * ins,
        out_specs=specs,
        scratch_shapes=scratch,
        compiler_params=params(24),
        cost_estimate=cost(count * arrays * 16 * 4 * V**3 * 2, 1 << 20),
    )(*amps, *facs, *held)


def couple_kernel(where_ref, sources_ref, weights_ref, flips_ref, near_ref, far_ref, out_ref, sums):
    sums[...] = jnp.zeros_like(sums)
    lane = lax.broadcasted_iota(jnp.int32, (V, 128), 1)

    def slot(s, none):
        p, k = s // 8, s % 8
        local = lax.rem(sources_ref[p, k], 2 * Y * ZL * C)
        side = lax.rem(local, 2)
        apart = (local // 2) ^ where_ref[0]
        core, rest = lax.rem(apart, 2), apart // 2
        flip = flips_ref[p, k]
        weight = weights_ref[p, k]
        mixed = jnp.where((lane // 64) == side, weight, 0.0)

        def gather(ref):
            main = ref[rest, :, pl.ds(pl.multiple_of(side * 128, 128), 128)].astype(jnp.float32)
            shared = ref[rest, :, 256:384].astype(jnp.float32)
            sums[p, flip, 0, 0:V, :] += weight * main
            sums[p, flip, 1, 0:V, :] += mixed * shared

        @pl.when(core == 0)
        def _():
            gather(near_ref)

        @pl.when(core == 1)
        def _():
            gather(far_ref)

        return none

    lax.fori_loop(0, 16, slot, 0)
    shared = []
    for p in range(2):
        plain, tail = sums[p, 0, 0, 0:V, :], sums[p, 0, 1, 0:V, :]
        tail = tail + turn(tail)
        turned_tail = sums[p, 1, 1]
        top = sums[p, 1, 0].T
        bottom = (turned_tail + turn(turned_tail)).T
        out_ref[0:128, 128 * p : 128 * p + 128] = plain[0:128] + top[:, 0:128]
        out_ref[128:V, 128 * p : 128 * p + 128] = plain[128:V] + bottom[0:64, 0:128]
        right = jnp.concatenate([top[:, 128:256], bottom[0:64, 128:256]], axis=0)
        shared.append(tail + (right if p == 0 else turn(right)))
    out_ref[:, 256:384] = jnp.where(lane < 64, shared[0], shared[1])


def couple(where, sources, weights, flips, near, far):
    return pl.pallas_call(
        couple_kernel,
        out_shape=jax.ShapeDtypeStruct((V, W), jnp.float32),
        in_specs=[SMEM] * 4 + [VMEM] * 2,
        out_specs=VMEM,
        scratch_shapes=[pltpu.VMEM((2, 2, 2, 256, 128), jnp.float32)],
        compiler_params=params(12),
        cost_estimate=cost(1 << 20, 4 << 20),
        name="couple",
    )(where, sources, weights, flips, near, far)


def finish_kernel(own_ref, couple_ref, a_ref, b_ref, c_ref, out_ref, total, flat):
    half = V // 2
    low = low_lanes(half)
    for t in range(3):
        cut = slice(128 * t, 128 * t + 128)
        total[t] = (own_ref[0, :, cut] + couple_ref[:, cut]) + (
            (a_ref[:, cut].astype(jnp.float32) + b_ref[:, cut].astype(jnp.float32))
            + c_ref[:, cut].astype(jnp.float32)
        )

    def line(t, odd):
        return total[t, pl.ds(odd, half, stride=2), :]

    for p in range(2):
        even, odd = line(2, 0), line(2, 1)
        main = turn(line(p, 1))
        flat[pl.ds(p, half, stride=24), :] = line(p, 0)
        flat[pl.ds(8 + p, half, stride=24), :] = jnp.where(low, even if p == 0 else turn(even), main)
        flat[pl.ds(16 + p, half, stride=24), :] = jnp.where(low, main, turn(odd) if p == 0 else odd)
    for k in range(TILES):
        out_ref[:, 128 * k : 128 * k + 128] = flat[8 * k : 8 * k + 2, :]


def finish(own, coupled, parts):
    return pl.pallas_call(
        finish_kernel,
        out_shape=jax.ShapeDtypeStruct((2, V * V), jnp.float32),
        in_specs=[VMEM] * 5,
        out_specs=VMEM,
        scratch_shapes=[
            pltpu.VMEM((3, V, 128), jnp.float32),
            pltpu.VMEM((8 * TILES, 128), jnp.float32),
        ],
        compiler_params=params(12),
        cost_estimate=cost(1 << 20, 2 << 20),
        name="finish",
    )(own, coupled, *parts)


def local(amplitudes, factors, sources, weights, flips):
    where = lax.axis_index("pair").astype(jnp.int32).reshape(1)

    def aux(value, mask):
        return lax.ppermute(value, "aux", aux_flip(mask))

    def pair(value, mask):
        return lax.ppermute(value, "pair", pair_flip(mask))

    pack = prep_amp(amplitudes)
    across, below, above = aux(pack, 2), aux(pack, 1), aux(pack, 3)
    own, other = prep_fac(where % C, factors)
    left, right = aux(own, ZH), aux(own, 3 * ZH)
    self_total = ladder([pack], [own, other], [], False, 4)
    held, left, right = lax.optimization_barrier((own, left, right))
    facing = aux(held, 2 * ZH)
    mates = jnp.stack([pack, pair(pack, 2)])
    rest = [across, below, above]
    total = ladder(rest, [own, other], [], False, 4)
    mates = jnp.concatenate([mates, pair(mates, 4)])
    sides_other = pair(jnp.concatenate([left, right]), 1)
    total = ladder(rest, [left, right], [(total, i) for i in range(3)], False, 4)
    near = jnp.concatenate([mates, pair(mates, 8)])
    total = ladder(rest, [sides_other], [(total, i) for i in range(3)], False, 4)
    facing_other = pair(facing, 1)
    total = ladder(rest, [facing], [(total, i) for i in range(3)], False, 4)
    far = pair(near, 1)
    back = ladder(rest, [facing_other], [(total, i) for i in range(3)], True, 4)
    parts = (aux(back[0], 2), aux(back[1], 1), aux(back[2], 3))
    facs = [left, right, sides_other, facing, facing_other]
    mine = ladder([pack], facs, [(self_total, 0)], False, 4)
    coupled = couple(where, sources, weights, flips, near, far)
    return finish(mine, coupled, parts)


def solution(mesh):
    placed = (
        P(("aux", "pair"), None),
        P("aux", None),
        P(("aux", "pair"), None),
        P(("aux", "pair"), None),
        P(("aux", "pair"), None),
    )
    return jax.shard_map(
        local, mesh=mesh, in_specs=placed, out_specs=P(("aux", "pair"), None), check_vma=False
    )
```
